32 devices in a mesh: grp: 8 (over z, core), tp: 4 (over y, x).
Axes of the slice: x: 2, y: 2, z: 4, core: 2. Of those that a mesh axis runs over, the one named last changes fastest.
Arguments:
- hidden: bfloat16 [128, 16384], P(('grp', 'tp')), may hold values from -130 to 130
- gain: float32 [16384], replicated, may hold values from 0.5 to 1.5
- head: bfloat16 [16384, 16384], P(None, ('grp', 'tp')), may hold values from -3 to 3
Outputs:
- log_probs: float32 [128, 16384], P(('grp', 'tp'))
The draws below stay inside these ranges and needn't reach their ends.
All inputs are finite; a program needn't handle non-finite values.
Results may differ from the reference program's by a relative error of at most 0.00055.
Values may be sent and summed in bfloat16 or wider, within the bound.
No kernel may reach another device: no remote copies, remote signals or barrier semaphores. Data moves between devices by JAX's collectives and lax.ppermute only.
A program may use at most 128 MiB of HBM per device.

```python
import math
import jax
import jax.numpy as jnp
from jax import lax

D = 16384
V_DEV = 512
TOK_DEV = 4
DEVICES = 32


def head_column(base, index):
    values = jax.random.normal(jax.random.fold_in(base, index), (D,), jnp.float32)
    return jnp.clip(values, -6.0, 6.0) * (3.0 / math.sqrt(D))


def draw_head(key, part):
    base = jax.random.fold_in(key, 11)
    columns = jax.vmap(lambda index: head_column(base, index))(jnp.arange(V_DEV * DEVICES))
    return columns.T.astype(jnp.bfloat16)


def draw_hidden(key, part):
    total_rows = TOK_DEV * DEVICES
    own_key = jax.random.fold_in(key, 23)
    row_scale = jnp.exp(jax.random.uniform(jax.random.fold_in(own_key, 1), (total_rows, 1), jnp.float32, 0.0, math.log(10.0)))
    col_scale = jnp.exp(jax.random.uniform(jax.random.fold_in(own_key, 2), (1, D), jnp.float32, 0.0, math.log(3.0)))
    rough = jnp.clip(jax.random.normal(jax.random.fold_in(own_key, 4), (total_rows, D), jnp.float32), -4.0, 4.0)
    values = rough * row_scale * col_scale
    return values.astype(jnp.bfloat16)


def setup_inputs(seed: int = 0) -> dict:
    splits = jax.random.split(jax.random.key(seed), 4)
    return {
        "hidden": draw_hidden(jax.random.fold_in(splits[3], 71), 0),
        "gain": jnp.clip(1.0 + 0.1 * jax.random.normal(splits[1], (D,), jnp.float32), 0.5, 1.5),
        "head": draw_head(jax.random.fold_in(splits[3], 71), 0),
    }


def reference(hidden, gain, head):
    values = hidden.astype(jnp.float32)
    mean_square = lax.optimization_barrier(jnp.mean(values * values, axis=-1, keepdims=True))
    normed = (values * lax.rsqrt(mean_square + 1e-05) * gain).astype(jnp.bfloat16)
    logits = jnp.dot(normed, head, preferred_element_type=jnp.float32)
    top = lax.optimization_barrier(jnp.max(logits, axis=-1, keepdims=True))
    total = lax.optimization_barrier(jnp.sum(jnp.exp(logits - top), axis=-1, keepdims=True))
    return logits - top - jnp.log(total)
```

```python
import jax
import jax.numpy as jnp
from jax import lax
from jax.experimental import pallas as pl
from jax.experimental.pallas import tpu as pltpu
from jax.sharding import PartitionSpec as P


AXES = ("grp", "tp")
EPS = 1e-05
PAD = 128
SCALE = 0.25
VMEM = pltpu.VMEM


def bits_between(low, high):
    bits = []
    while low < high:
        bits.append(low)
        low *= 2
    assert low == high
    return bits


def interleave(a, b):
    mixed = []
    for i in range(max(len(a), len(b))):
        mixed += a[i : i + 1] + b[i : i + 1]
    return mixed


def plan(groups, tp):
    near = bits_between(1, tp)
    far = bits_between(2 * tp, groups * tp)[::-1]
    back = near[::-1]
    return [
        (10, (far + near, far + back)),
        (6, (interleave(near, far), interleave(back, far))),
    ]


def vmem_spec():
    return pl.BlockSpec(memory_space=VMEM)


def in_vmem(x):
    return pltpu.with_memory_space_constraint(x, VMEM)


def in_hbm(x):
    return pltpu.with_memory_space_constraint(x, pltpu.HBM)


def norm_kernel(own_ref, other_ref, gain_ref, *out_refs):
    width = own_ref.shape[1]
    core = lax.rem(lax.axis_index("grp"), 2)
    half = width // 2
    own, other = own_ref[...].astype(jnp.float32), other_ref[...].astype(jnp.float32)
    mine = core == 0
    values = jnp.concatenate([jnp.where(mine, own, other), jnp.where(mine, other, own)], axis=0)
    mean_square = jnp.mean(values * values, axis=-1, keepdims=True)
    scale = lax.rsqrt(mean_square + EPS)
    start = 0
    for out_ref in out_refs:
        span = out_ref.shape[1]
        columns = pl.ds(pl.multiple_of(core * half + start, 128), span)
        part = jnp.where(mine, values[:, start : start + span], values[:, half + start : half + start + span])
        out_ref[...] = (part * scale * gain_ref[:, columns]).astype(jnp.bfloat16)
        start += span


def prep_kernel(hidden_ref, gain_ref, hidden_out, gain_out, sems):
    copies = [
        pltpu.make_async_copy(hidden_ref, hidden_out, sems.at[0]),
        pltpu.make_async_copy(gain_ref, gain_out, sems.at[1]),
    ]
    for copy in copies:
        copy.start()
    for copy in copies:
        copy.wait()


def prep(hidden, gain):
    gain = gain.reshape(1, -1)
    return pl.pallas_call(
        prep_kernel,
        out_shape=[jax.ShapeDtypeStruct(x.shape, x.dtype) for x in (hidden, gain)],
        in_specs=[pl.BlockSpec(memory_space=pltpu.HBM)] * 2,
        out_specs=[vmem_spec()] * 2,
        scratch_shapes=[pltpu.SemaphoreType.DMA((2,))],
        compiler_params=pltpu.CompilerParams(vmem_limit_bytes=2 << 20),
        cost_estimate=pl.CostEstimate(flops=0, bytes_accessed=4 * hidden.size, transcendentals=0),
        name="prep",
    )(in_hbm(hidden), in_hbm(gain))


def norm(hidden, other, gain, widths):
    tokens = hidden.shape[0]
    return pl.pallas_call(
        norm_kernel,
        out_shape=[jax.ShapeDtypeStruct((2 * tokens, w), jnp.bfloat16) for w in widths],
        in_specs=[vmem_spec()] * 3,
        out_specs=[vmem_spec()] * len(widths),
        compiler_params=pltpu.CompilerParams(vmem_limit_bytes=6 << 20),
        cost_estimate=pl.CostEstimate(flops=10 * hidden.size, bytes_accessed=4 * hidden.size, transcendentals=0),
        name="norm",
    )(hidden, other, gain)


def chip_offsets(bits, count):
    offsets = []
    for r in range(count):
        offset = 0
        for s, bit in enumerate(bits):
            if (r >> s) & 1:
                offset = offset ^ bit
        offsets.append(offset)
    return offsets


def add_blocks(tp, acc_ref, total, offsets, k_core, fresh):
    grp, t = lax.axis_index("grp"), lax.axis_index("tp")
    here = (grp - lax.rem(grp, 2)) * tp + t
    block = acc_ref.shape[1]
    for r, (off0, off1) in enumerate(offsets):
        chip = here ^ (off0 if off0 == off1 else off0 + k_core * (off1 - off0))
        slot = (chip // (2 * tp)) * tp + chip % tp
        value = total[r * block : (r + 1) * block, :]
        if fresh:
            acc_ref[slot] = value
        else:
            acc_ref[slot] += value


def head_kernel(tp, terms, last, fresh, *refs):
    refs = list(refs)
    pieces = refs[: len(terms)]
    head_ref = refs[len(terms)]
    if last:
        acc_in, out_ref, acc_ref = refs[len(terms) + 1 :]
        acc_ref[...] = acc_in[...]
    else:
        acc_ref = refs[-1]
    core = lax.rem(lax.axis_index("grp"), 2)
    half = head_ref.shape[0] // 2
    if fresh:
        acc_ref[...] = jnp.zeros_like(acc_ref)
    for ref, (start, offsets, own) in zip(pieces, terms):
        k_core = core if own else 1 - core
        span = ref.shape[1]
        step = min(span, 1024)
        while span % step:
            step //= 2
        total = None
        for k in range(0, span, step):
            rows = pl.ds(pl.multiple_of(k_core * half + start + k, 128), step)
            part = jnp.dot(ref[:, k : k + step], head_ref[rows, :], preferred_element_type=jnp.float32)
            total = part if total is None else total + part
        add_blocks(tp, acc_ref, total, offsets, k_core, False)
    if last:
        chips, block, width = acc_ref.shape
        tokens = block // 2
        for q in range(chips):
            logits = acc_ref[q]
            top = jnp.max(logits, axis=-1, keepdims=True)
            lse = top + jnp.log(jnp.sum(jnp.exp(logits - top), axis=-1, keepdims=True))
            sent = (logits - lse) * SCALE
            scaled = lse * SCALE
            high = jnp.floor(scaled / 16 + 0.5) * 16
            mid = jnp.floor((scaled - high) * 64 + 0.5) / 64
            low = scaled - high - mid
            lane = lax.broadcasted_iota(jnp.int32, (block, PAD), 1)
            tail = jnp.where(lane == 0, high, jnp.where(lane == 1, mid, low))
            d = (q // tp) * 2 * tp + q % tp
            for c in range(2):
                out_ref[d + c * tp, :, :width] = sent[c * tokens : (c + 1) * tokens]
                out_ref[d + c * tp, :, width:] = tail[c * tokens : (c + 1) * tokens]


def head_part(tp, chips, block, pieces, terms, head, acc, last=False):
    width = head.shape[1]
    acc_shape = (chips, block, width)
    fresh = acc is None
    args = [in_vmem(p) for p in pieces] + [head] + ([] if fresh else [acc])

    def kernel(*refs):
        head_kernel(tp, terms, last, fresh, *refs)

    if last:
        out = jax.ShapeDtypeStruct((2 * chips, block // 2, width + PAD), jnp.float32)
    else:
        out = jax.ShapeDtypeStruct(acc_shape, jnp.float32)
    work = sum(p.size for p in pieces)
    return pl.pallas_call(
        kernel,
        out_shape=out,
        in_specs=[vmem_spec()] * len(args),
        out_specs=vmem_spec(),
        scratch_shapes=[VMEM(acc_shape, jnp.float32)] if last else [],
        input_output_aliases={} if fresh or last else {len(args) - 1: 0},
        compiler_params=pltpu.CompilerParams(vmem_limit_bytes=8 << 20),
        cost_estimate=pl.CostEstimate(flops=2 * work * width, bytes_accessed=2 * work, transcendentals=0),
        name="head",
    )(*args)


def load_kernel(head_ref, out_ref, sem):
    copy = pltpu.make_async_copy(head_ref, out_ref, sem)
    copy.start()
    copy.wait()


def load(head):
    return pl.pallas_call(
        load_kernel,
        out_shape=jax.ShapeDtypeStruct(head.shape, head.dtype),
        in_specs=[pl.BlockSpec(memory_space=pltpu.HBM)],
        out_specs=vmem_spec(),
        scratch_shapes=[pltpu.SemaphoreType.DMA],
        compiler_params=pltpu.CompilerParams(vmem_limit_bytes=2 << 20),
        cost_estimate=pl.CostEstimate(flops=0, bytes_accessed=2 * head.size, transcendentals=0),
        name="load",
    )(in_hbm(head))


def finish_kernel(got_ref, out_ref):
    devices, _, wide = got_ref.shape
    width = wide - PAD
    parts = got_ref[:, :, width : width + PAD]
    lse = (parts[:, :, 0:1] + parts[:, :, 1:2] + parts[:, :, 2:3]) / SCALE
    top = jnp.max(lse, axis=0, keepdims=True)
    whole = top + jnp.log(jnp.sum(jnp.exp(lse - top), axis=0, keepdims=True))
    shift = lse - whole
    for d in range(devices):
        out_ref[:, d * width : (d + 1) * width] = got_ref[d, :, :width] / SCALE + shift[d]


def finish(got, width):
    devices, tokens, _ = got.shape
    return pl.pallas_call(
        finish_kernel,
        out_shape=jax.ShapeDtypeStruct((tokens, devices * width), jnp.float32),
        in_specs=[vmem_spec()],
        out_specs=vmem_spec(),
        compiler_params=pltpu.CompilerParams(vmem_limit_bytes=8 << 20),
        name="finish",
    )(got)


def solution(mesh):
    groups, tp = mesh.shape["grp"], mesh.shape["tp"]
    devices = groups * tp
    pair = [(i, i ^ tp) for i in range(devices)]

    def stage(bit0, bit1):
        return [(i, i ^ (bit1 if i & tp else bit0)) for i in range(devices)]

    chunks = plan(groups, tp)
    count = len(chunks[0][1][0])
    chips = devices // 2
    offsets = [list(zip(*(chip_offsets(o, chips) for o in orders))) for _, orders in chunks]
    near = [o[: chips // 2] for o in offsets]
    far = [o[chips // 2 :] for o in offsets]
    every = range(len(chunks))
    final = len(chunks) - 1

    def permute(x, pairs):
        return lax.ppermute(x, AXES, pairs)

    def on_device(hidden, gain, head):
        half = hidden.shape[1] // 2
        block = 2 * hidden.shape[0]
        widths = [share * half // 16 for share, _ in chunks]
        starts = [sum(widths[:j]) for j in every]
        head_here = load(head)
        other = permute(hidden, pair)
        hidden, gain = prep(hidden, gain)
        bufs = list(norm(hidden, other, gain, widths))
        recvs = [None] * len(chunks)
        for s in range(count):
            for j, (_, orders) in enumerate(chunks):
                recvs[j] = permute(bufs[j], stage(orders[0][s], orders[1][s]))
            if s < count - 1:
                for j in every:
                    bufs[j] = jnp.concatenate([bufs[j], recvs[j]], axis=0)

        def part(pieces, terms, acc, last=False):
            return head_part(tp, chips, block, pieces, terms, head_here, acc, last)

        acc = None
        for j in every:
            pieces = [bufs[j], permute(bufs[j], pair)]
            acc = part(pieces, [(starts[j], near[j], True), (starts[j], near[j], False)], acc)
        mirrored = [permute(recvs[j], pair) for j in every]
        for j in every:
            acc = part([recvs[j]], [(starts[j], far[j], True)], acc)
        for j in every:
            acc = part([mirrored[j]], [(starts[j], far[j], False)], acc, last=j == final)
        got = lax.all_to_all(acc.astype(jnp.float16), AXES, split_axis=0, concat_axis=0, tiled=True)
        return finish(got.astype(jnp.float32), head.shape[1])

    return jax.shard_map(
        on_device,
        mesh=mesh,
        in_specs=(P(AXES, None), P(), P(None, AXES)),
        out_specs=P(AXES, None),
        check_vma=False,
    )
```
